128 devices in a mesh: seq: 32 (over x, z, core), head: 4 (over y).
Axes of the slice: x: 4, y: 4, z: 4, core: 2. Of those that a mesh axis runs over, the one named last changes fastest.
Arguments:
- hidden_in: bfloat16 [4096, 2048], P('seq', 'head'), may hold values from -6 to 6
- out_grad: float32 [4096, 2048], P('seq', 'head'), may hold values from -6 to 6
- expert_ids: int32 [4096, 8], P('seq'), may hold values from 0 to 63, all different within a row; in each aligned block of 128 rows (0 to 127, 128 to 255, ...) at most 32 rows name the same one
- route_weights: float32 [4096, 8], P('seq'), may hold values from 0.03 to 0.3
- w_gate: bfloat16 [64, 2048, 1024], P('seq', None, 'head'), may hold values from -0.125 to 0.125
- w_up: bfloat16 [64, 2048, 1024], P('seq', None, 'head'), may hold values from -0.125 to 0.125
- w_down: bfloat16 [64, 1024, 2048], P('seq', 'head'), may hold values from -0.1875 to 0.1875
- query_in: float32 [4096, 2048], P('seq', 'head'), may hold values from -6 to 6
- key_in: float32 [4096, 2048], P('seq', 'head'), may hold values from -6 to 6
- value_in: float32 [4096, 2048], P('seq', 'head'), may hold values from -6 to 6
- state_before: float32 [16, 128, 128], P('head'), may hold values from -384 to 384
- grad_after: float32 [16, 128, 128], P('head'), may hold values from -384 to 384
Outputs:
- grad_gate: bfloat16 [64, 2048, 1024], P('seq', None, 'head')
- grad_up: bfloat16 [64, 2048, 1024], P('seq', None, 'head')
- grad_down: bfloat16 [64, 1024, 2048], P('seq', 'head')
- grad_query: float32 [4096, 2048], P('seq', 'head')
- grad_key: float32 [4096, 2048], P('seq', 'head')
- grad_value: float32 [4096, 2048], P('seq', 'head')
The draws below stay inside these ranges and needn't reach their ends.
Inputs may be any that keep to these rules, and one draw needn't show every extreme that they name: `expert_ids`: each row names 8 different experts. Among the 128 rows of one index of seq (aligned blocks of 128 rows) no expert is named more than 32 times, a bound that some block reaches.
All inputs are finite; a program needn't handle non-finite values.
Results may differ from the reference program's by a relative error of at most 0.014.
Values may be sent and summed in bfloat16 or wider, within the bound.
No kernel may reach another device: no remote copies, remote signals or barrier semaphores. Data moves between devices by JAX's collectives and lax.ppermute only.
A program may use at most 128 MiB of HBM per device.

```python
import math
import jax
import jax.numpy as jnp
import numpy as np
from jax import lax

D = 2048
FF = 1024
EXPERTS = 64
TOPK = 8
HEADS = 16
HD = 128
TOK_DEV = 128
TOKENS = 4096
CAP = 32
N_SEQ = 32
N_HEAD = 4


def steps_of(own_key, extent, shards, least, high):
    factor_of = 1.0
    for position, blocks in shards:
        draws = jax.random.uniform(jax.random.fold_in(jax.random.fold_in(own_key, 6), position), (blocks,), jnp.float32, least / len(shards), high / len(shards))
        factor_of = factor_of * jnp.repeat(jnp.exp(draws), extent[position] // blocks).reshape((-1,) + (1,) * (len(extent) - 1 - position))
    return factor_of


def routed_block(own_key, own, number, rows, number_of, top, limit, lean):
    order = jax.random.permutation(own_key, number_of)
    crowded, common = load_shares(number_of, rows * top, limit, lean, True), load_shares(number_of, rows * top, limit, lean, False)
    places = jnp.arange(number_of)

    def named(sizes, offset_by):
        used = int((sizes > 0).sum())
        fixed = max(1, used // 4)
        passed = fixed + (places - fixed + offset_by * (used - fixed)) % max(1, number_of - fixed)
        return jnp.zeros((number_of,), jnp.int32).at[order[jnp.where(places < fixed, places, passed)]].set(jnp.asarray(sizes, jnp.int32))

    sizes = jnp.where(number % 4 == 0, named(crowded, number // 4), named(common, number - number // 4 - 1))
    mixed = jax.random.permutation(jax.random.fold_in(own, 3), number_of)
    source_of, receiver = mixed[0:number_of // 2 * 2:2], mixed[1:number_of // 2 * 2:2]
    slack = jnp.minimum(sizes[source_of] - 1, limit - sizes[receiver]) // 2
    slack = jnp.where((source_of == order[0]) | (receiver == order[0]) | (sizes[receiver] == 0), 0, jnp.maximum(slack, 0))
    passed = jax.random.randint(jax.random.fold_in(own, 4), (number_of // 2,), 0, 1 << 20) % (slack + 1)
    sizes = sizes.at[source_of].add(-passed).at[receiver].add(passed)
    labels = jnp.searchsorted(jnp.cumsum(sizes), jnp.arange(rows * top), side="right").astype(jnp.int32)
    table = labels.reshape(top, rows).T
    table = table[jax.random.permutation(jax.random.fold_in(own, 1), rows)]
    offset_by = jax.random.randint(jax.random.fold_in(own, 2), (rows, 1), 0, top)
    return jnp.take_along_axis(table, (jnp.arange(top)[None, :] + offset_by) % top, axis=1)


def load_shares(amount, total, limit, skew, full):
    loads = [(1 << 20) // math.isqrt(rank ** skew) + 1 for rank in range(1, amount + 1)]
    largest = limit if full else min(limit, max(-(-total // amount), total * loads[0] // sum(loads)))
    least = 1 if total - largest >= amount - 1 else 0
    holding, spare = [largest] + [least] * (amount - 1), total - largest - least * (amount - 1)
    while spare > 0:
        candidates = [i for i in range(1, amount) if holding[i] < largest] or [i for i in range(1, amount) if holding[i] < limit]
        whole, remaining = sum([loads[i] for i in candidates]), spare
        for i in candidates:
            addition = min(limit - holding[i], max(1, remaining * loads[i] // whole), spare)
            holding[i] = holding[i] + addition
            spare = spare - addition
    return np.array(holding)


def noise(own_key, extent, spread, bound, shards=(), kind=jnp.bfloat16):
    values = spread * jax.random.normal(own_key, extent, jnp.float32)
    if shards:
        values = values * steps_of(own_key, extent, shards, -0.22, 0.18)
    return jnp.clip(values, -bound, bound).astype(kind)


def setup_inputs(seed: int = 0) -> dict:
    key_list = jax.random.split(jax.random.key(seed), 13)
    hidden_in = noise(key_list[0], (TOKENS, D), 1.0, 6.0, ((0, 32), (1, 4)))
    out_grad = noise(key_list[1], (TOKENS, D), 1.0, 6.0, ((0, 32), (1, 4)), jnp.float32)
    expert_ids_keys = jax.random.split(jax.random.fold_in(key_list[2], 1), TOKENS // TOK_DEV)
    expert_ids_turns = jax.random.permutation(jax.random.fold_in(key_list[2], 3), TOKENS // TOK_DEV)
    expert_ids = jax.vmap(lambda own, number: routed_block(jax.random.fold_in(key_list[2], 2), own, number, TOK_DEV, EXPERTS, TOPK, CAP, 2))(expert_ids_keys, expert_ids_turns).reshape((TOKENS, TOPK))
    route_weights = jnp.clip(jnp.exp(math.log(0.3) - 2.3025852 * jax.random.uniform(key_list[3], (TOKENS, TOPK), jnp.float32) ** steps_of(key_list[3], (TOKENS, TOPK), ((0, 32),), -0.2, 0.2)), 0.03, 0.3)
    w_gate = noise(key_list[4], (EXPERTS, D, FF), D ** -0.5, 0.125, ((0, 32), (2, 4)))
    w_up = noise(key_list[5], (EXPERTS, D, FF), D ** -0.5, 0.125, ((0, 32), (2, 4)))
    w_down = noise(key_list[6], (EXPERTS, FF, D), FF ** -0.5, 0.1875, ((0, 32), (1, 4)))
    query_in = noise(key_list[7], (TOKENS, D), 1.0, 6.0, ((0, 32), (1, 4)), jnp.float32)
    key_in = noise(key_list[8], (TOKENS, D), 1.0, 6.0, ((0, 32), (1, 4)), jnp.float32)
    value_in = noise(key_list[9], (TOKENS, D), 1.0, 6.0, ((0, 32), (1, 4)), jnp.float32)
    state_before = noise(key_list[10], (HEADS, HD, HD), (TOKENS ** 0.5), 384.0, ((0, 4),), jnp.float32)
    grad_after = noise(key_list[11], (HEADS, HD, HD), (TOKENS ** 0.5), 384.0, ((0, 4),), jnp.float32)
    return {"hidden_in": hidden_in, "out_grad": out_grad, "expert_ids": expert_ids, "route_weights": route_weights, "w_gate": w_gate, "w_up": w_up, "w_down": w_down, "query_in": query_in, "key_in": key_in, "value_in": value_in, "state_before": state_before, "grad_after": grad_after}


HIGHEST = lax.Precision.HIGHEST


def attention_backward(query_in, key_in, value_in, attn_grad, prefix, suffix, attn_scale):
    block_len = query_in.shape[0]
    causal = jnp.arange(block_len)[:, None] >= jnp.arange(block_len)[None, :]
    score_grad = jnp.einsum("thj,shj->hts", attn_grad, value_in, precision=HIGHEST)
    score_grad = jnp.where(causal[None], score_grad, 0.0)
    score_match = jnp.einsum("thi,shi->hts", query_in, key_in, precision=HIGHEST)
    score_match = jnp.where(causal[None], score_match, 0.0)
    grad_query = jnp.einsum("hts,shi->thi", score_grad, key_in, precision=HIGHEST)
    grad_query = grad_query + jnp.einsum("thj,hij->thi", attn_grad, prefix, precision=HIGHEST)
    grad_key = jnp.einsum("hts,thi->shi", score_grad, query_in, precision=HIGHEST)
    grad_key = grad_key + jnp.einsum("shj,hij->shi", value_in, suffix, precision=HIGHEST)
    grad_value = jnp.einsum("hts,thj->shj", score_match, attn_grad, precision=HIGHEST)
    grad_value = grad_value + jnp.einsum("shi,hij->shj", key_in, suffix, precision=HIGHEST)
    return grad_query * attn_scale, grad_key * attn_scale, grad_value * attn_scale


def expert_reference(row_data, grad_rows, gate_mat, up_mat, down_mat):
    row_wide = row_data.astype(jnp.float32)
    grad_wide = grad_rows.astype(jnp.float32)
    gate_wide = gate_mat.astype(jnp.float32)
    up_wide = up_mat.astype(jnp.float32)
    down_wide = down_mat.astype(jnp.float32)
    pre_gate = jnp.dot(row_wide, gate_wide, precision=HIGHEST)
    pre_up = jnp.dot(row_wide, up_wide, precision=HIGHEST)
    gate_sigmoid = jax.nn.sigmoid(pre_gate)
    gate_swish = pre_gate * gate_sigmoid
    hidden_act = (gate_swish * pre_up).astype(jnp.bfloat16)
    d_inner = jnp.dot(grad_wide, down_wide.T, precision=HIGHEST)
    d_gate = (d_inner * pre_up * gate_sigmoid * (1.0 + pre_gate * (1.0 - gate_sigmoid))).astype(jnp.bfloat16)
    d_up = (d_inner * gate_swish).astype(jnp.bfloat16)
    grad_down = jnp.dot(hidden_act.astype(jnp.float32).T, grad_wide, precision=HIGHEST)
    grad_gate = jnp.dot(row_wide.T, d_gate.astype(jnp.float32), precision=HIGHEST)
    grad_up = jnp.dot(row_wide.T, d_up.astype(jnp.float32), precision=HIGHEST)
    group_width = FF // N_HEAD
    gate_split = gate_wide.reshape(D, N_HEAD, group_width)
    up_split = up_wide.reshape(D, N_HEAD, group_width)
    dgate_split = d_gate.astype(jnp.float32).reshape(-1, N_HEAD, group_width)
    dup_split = d_up.astype(jnp.float32).reshape(-1, N_HEAD, group_width)
    group_part = jnp.einsum("rqf,dqf->qrd", dgate_split, gate_split, precision=HIGHEST)
    group_part = group_part + jnp.einsum("rqf,dqf->qrd", dup_split, up_split, precision=HIGHEST)
    group_round = lax.optimization_barrier(group_part.astype(jnp.bfloat16))
    hidden_part = jnp.sum(group_round.astype(jnp.float32), axis=0)
    return grad_gate.astype(jnp.bfloat16), grad_up.astype(jnp.bfloat16), grad_down.astype(jnp.bfloat16), hidden_part


def reference(hidden_in, out_grad, expert_ids, route_weights, w_gate, w_up, w_down, query_in, key_in, value_in, state_before, grad_after):
    slot_total = N_SEQ * CAP
    flat_ids = expert_ids.reshape(-1)
    onehot = (flat_ids[:, None] == jnp.arange(EXPERTS, dtype=jnp.int32)[None, :]).astype(jnp.int32)
    slot_rank = jnp.sum((jnp.cumsum(onehot, axis=0) - onehot) * onehot, axis=1)
    slot_dest = flat_ids * slot_total + slot_rank
    pair_token = jnp.arange(TOKENS * TOPK, dtype=jnp.int32) // TOPK
    slot_token = jnp.zeros((EXPERTS * slot_total,), jnp.int32).at[slot_dest].set(pair_token)
    slot_weight = jnp.zeros((EXPERTS * slot_total,), jnp.float32).at[slot_dest].set(route_weights.reshape(-1))
    slot_token = slot_token.reshape(EXPERTS, slot_total)
    slot_weight = slot_weight.reshape(EXPERTS, slot_total)

    def one_expert(running_sum, inputs):
        token_ids, pair_weight, gate_mat, up_mat, down_mat = inputs
        row_data = hidden_in[token_ids]
        grad_rows = (pair_weight[:, None] * out_grad[token_ids]).astype(jnp.bfloat16)
        grad_gate, grad_up, grad_down, hidden_part = expert_reference(row_data, grad_rows, gate_mat, up_mat, down_mat)
        running_sum = running_sum.at[token_ids].add(hidden_part)
        return running_sum, (grad_gate, grad_up, grad_down)

    moe_grad, weight_grads = lax.scan(one_expert, jnp.zeros((TOKENS, D), jnp.float32), (slot_token, slot_weight, w_gate, w_up, w_down))
    grad_gate, grad_up, grad_down = weight_grads

    attn_grad = out_grad + moe_grad
    shape_four = (N_SEQ, TOK_DEV, HEADS, HD)
    query_blocks = query_in.reshape(shape_four)
    key_blocks = key_in.reshape(shape_four)
    value_blocks = value_in.reshape(shape_four)
    grad_blocks = attn_grad.reshape(shape_four)
    kv_local = jnp.einsum("cshi,cshj->chij", key_blocks, value_blocks, precision=HIGHEST)
    qd_local = jnp.einsum("cthi,cthj->chij", query_blocks, grad_blocks, precision=HIGHEST)
    zero_state = jnp.zeros((1, HEADS, HD, HD), jnp.float32)
    prefix = jnp.concatenate([zero_state, jnp.cumsum(kv_local, axis=0)[:-1]], axis=0) + state_before[None]
    later_sum = jnp.cumsum(qd_local[::-1], axis=0)[::-1]
    suffix = jnp.concatenate([later_sum[1:], zero_state], axis=0) + grad_after[None]
    attn_scale = (HD * TOKENS) ** -0.5
    grad_query, grad_key, grad_value = jax.vmap(attention_backward, in_axes=(0, 0, 0, 0, 0, 0, None))(
        query_blocks, key_blocks, value_blocks, grad_blocks, prefix, suffix, attn_scale)
    return (grad_gate, grad_up, grad_down, grad_query.reshape(TOKENS, D), grad_key.reshape(TOKENS, D), grad_value.reshape(TOKENS, D))
```

```python
import jax
import jax.numpy as jnp
from jax import lax
from jax.experimental import pallas as pl
from jax.experimental.pallas import tpu as pltpu
from jax.sharding import Mesh
from jax.sharding import PartitionSpec as P

HD = 128
CAP = 32
TOK = 128
QW = 512
FFQ = 256
BLOCKS = 16
SLOTS = 128
INFO = 16
SEQ = ("x", "z", "c")
PLANE = ("x", "z", "y")
ROWS = ((0, 48), (48, 48), (96, 32))
HIGHEST = lax.Precision.HIGHEST
BF = jnp.bfloat16
F32 = jnp.float32


def shift(a, axis, s):
    return lax.ppermute(a, axis, [(i, (i + s) % 4) for i in range(4)])


def swap(a):
    return lax.ppermute(a, "c", [(0, 1), (1, 0)])


def entering(local, reverse):
    core = lax.axis_index("c")
    other = swap(local.astype(BF)).astype(F32)
    before = jnp.where((core == 0) if reverse else (core == 1), other, 0.0)
    total = local + other
    for axis in ("z", "x"):
        index = lax.axis_index(axis)
        sent = total.astype(BF)
        got = [shift(sent, axis, s).astype(F32) for s in (1, 2, 3)]
        for s in (1, 2, 3):
            passed = (index < s) if reverse else (index >= s)
            before = before + jnp.where(passed, got[s - 1], 0.0)
        total = total + got[0] + got[1] + got[2]
    return before


def dot(a, b, ca, cb):
    return lax.dot_general(a, b, (((ca,), (cb,)), ((), ())), preferred_element_type=F32)


def expert_kernel(place, eids, tok, wg0, wg1, wu0, wu1, wd0, wd1, *rest):
    outs = rest[:12]
    xo, go, dgo, duo, hao = rest[12:17]
    hbuf, gbuf, pbuf, ibuf, wg, wu, wd, hot, wsl, act, sem_t, sem_w, sem_o, sem_p = rest[17:]
    px, pz, py = place[0], place[1], place[2]

    def weight_copies():
        for own, (a, b) in enumerate(((wg0, wg1), (wu0, wu1), (wd0, wd1))):
            dst = (wg, wu, wd)[own]
            yield pltpu.make_async_copy(a, dst.at[pl.ds(0, 2)], sem_w.at[2 * own])
            yield pltpu.make_async_copy(b, dst.at[pl.ds(2, 2)], sem_w.at[2 * own + 1])

    def token_copies(j):
        src = tok.at[pl.ds(4 * j, 4)]
        return (
            pltpu.make_async_copy(src.at[:, pl.ds(0, TOK), :], hbuf.at[j], sem_t.at[0, j]),
            pltpu.make_async_copy(src.at[:, pl.ds(TOK, TOK), :], gbuf.at[j], sem_t.at[1, j]),
            pltpu.make_async_copy(
                tok.at[4 * j, pl.ds(2 * TOK, INFO), pl.ds(0, 256)], ibuf.at[j], sem_t.at[2, j]
            ),
        )

    def start_tokens(j, carry):
        for cp in token_copies(j):
            cp.start()
        return carry

    lax.fori_loop(0, BLOCKS, start_tokens, 0)
    for cp in weight_copies():
        cp.start()

    row = lax.broadcasted_iota(jnp.int32, (TOK, TOK), 0)
    col = lax.broadcasted_iota(jnp.int32, (TOK, TOK), 1)
    upper = jnp.where(row < col, 1.0, 0.0).astype(BF)
    slot32 = lax.broadcasted_iota(jnp.int32, (CAP, TOK), 0).astype(F32)

    def select(j, carry):
        for cp in token_copies(j):
            cp.wait()
        info = ibuf[j].astype(F32)
        ids = info[0:8, 0:128]
        weights = info[8:16, 0:128] + info[0:8, 128:256]
        masks = []
        values = []
        for k in range(4):
            hit = ids == eids[k].astype(F32)
            masks.append(jnp.sum(jnp.where(hit, 1.0, 0.0), axis=0, keepdims=True))
            values.append(jnp.sum(jnp.where(hit, weights, 0.0), axis=0, keepdims=True))
        mask = jnp.concatenate(masks + masks, axis=0)
        rank = dot(mask.astype(BF), upper, 1, 0)
        parts = []
        slot_w = []
        for k in range(4):
            pick = (slot32 == rank[k : k + 1, :]) & (mask[k : k + 1, :] > 0.5)
            parts.append(jnp.where(pick, 1.0, 0.0))
            slot_w.append(
                jnp.sum(jnp.where(pick, values[k], 0.0), axis=1, keepdims=True)
            )
        onehot = jnp.concatenate(parts, axis=0).astype(BF)
        hot[j] = onehot
        wsl[j] = jnp.broadcast_to(jnp.concatenate(slot_w, axis=0), (SLOTS, 128))
        for y in range(4):
            hbuf[j, y] = dot(onehot, hbuf[j, y], 1, 0).astype(BF)
            gbuf[j, y] = dot(onehot, gbuf[j, y], 1, 0).astype(BF)
        pltpu.make_async_copy(hbuf.at[j], xo.at[j], sem_o.at[0]).start()
        pltpu.make_async_copy(gbuf.at[j], go.at[j], sem_o.at[1]).start()
        return carry

    lax.fori_loop(0, BLOCKS, select, 0)
    for cp in weight_copies():
        cp.wait()

    def expert(k, carry):
        r0 = pl.multiple_of(k * CAP, CAP)
        gate = jnp.zeros((BLOCKS * CAP, FFQ), F32)
        up = jnp.zeros((BLOCKS * CAP, FFQ), F32)
        inner = jnp.zeros((BLOCKS * CAP, FFQ), F32)
        for y in range(4):
            x = hbuf[:, y, pl.ds(r0, CAP), :].reshape(BLOCKS * CAP, QW)
            g = gbuf[:, y, pl.ds(r0, CAP), :].reshape(BLOCKS * CAP, QW)
            gate = gate + dot(x, wg[k, y * QW : (y + 1) * QW, :], 1, 0)
            up = up + dot(x, wu[k, y * QW : (y + 1) * QW, :], 1, 0)
            inner = inner + dot(g, wd[k, :, y * QW : (y + 1) * QW], 1, 1)
        w = wsl[:, pl.ds(r0, CAP), :].reshape(BLOCKS * CAP, 128)
        w = jnp.concatenate([w, w], axis=1)
        sig = 1.0 / (1.0 + jnp.exp(-gate))
        swish = gate * sig
        inner = inner * w
        dg = (inner * up * sig * (1.0 + gate * (1.0 - sig))).astype(BF)
        du = (inner * swish).astype(BF)
        act[0, k] = dg
        act[1, k] = du
        act[2, k] = (swish * up * w).astype(BF)
        for y in range(4):
            part = dot(dg, wg[k, y * QW : (y + 1) * QW, :], 1, 1)
            part = part + dot(du, wu[k, y * QW : (y + 1) * QW, :], 1, 1)
            pbuf[:, y, pl.ds(r0, CAP), :] = part.astype(BF).reshape(BLOCKS, CAP, QW)
        return carry

    lax.fori_loop(0, 4, expert, 0)
    act_copies = [
        pltpu.make_async_copy(act.at[n], (dgo, duo, hao)[n], sem_p.at[n]) for n in range(3)
    ]
    for cp in act_copies:
        cp.start()

    def out_copies(sx, sz, j):
        for sy in range(4):
            y = (py + sy) % 4
            for n, (r, size) in enumerate(ROWS):
                src = pbuf.at[j, y, pl.ds(r, size), :]
                if n == 0:
                    dst = outs[sx].at[sz, sy]
                elif n == 1:
                    dst = outs[4 + sz].at[sy, sx]
                else:
                    dst = outs[8 + sy].at[sx, sz]
                yield pltpu.make_async_copy(src, dst, sem_o.at[2])

    for sx in range(4):
        for sz in range(4):
            j = ((px + sx) % 4) * 4 + (pz + sz) % 4
            onehot = hot[j]
            for y in range(4):
                pbuf[j, y] = dot(onehot, pbuf[j, y], 0, 0).astype(BF)
            for cp in out_copies(sx, sz, j):
                cp.start()
    pltpu.make_async_copy(hbuf, xo, sem_o.at[0]).wait()
    pltpu.make_async_copy(gbuf, go, sem_o.at[1]).wait()
    pltpu.make_async_copy(pbuf, pbuf, sem_o.at[2]).wait()
    for cp in act_copies:
        cp.wait()


def run_experts(place, eids, tok, own, partner):
    any_spec = pl.BlockSpec(memory_space=pl.ANY)
    smem = pl.BlockSpec(memory_space=pltpu.SMEM)
    slabs = [
        jax.ShapeDtypeStruct((4, 4, size, QW), BF) for _, size in ROWS for _ in range(4)
    ]
    grid_shape = (BLOCKS, 4, TOK, QW)
    kept = [jax.ShapeDtypeStruct(grid_shape, BF)] * 2 + [
        jax.ShapeDtypeStruct((4, BLOCKS * CAP, FFQ), BF)
    ] * 3
    out = pl.pallas_call(
        expert_kernel,
        out_shape=slabs + kept,
        in_specs=[smem, smem] + [any_spec] * 7,
        out_specs=[any_spec] * 17,
        scratch_shapes=[
            pltpu.VMEM(grid_shape, BF),
            pltpu.VMEM(grid_shape, BF),
            pltpu.VMEM(grid_shape, BF),
            pltpu.VMEM((BLOCKS, INFO, 256), BF),
            pltpu.VMEM((4, 2048, FFQ), BF),
            pltpu.VMEM((4, 2048, FFQ), BF),
            pltpu.VMEM((4, FFQ, 2048), BF),
            pltpu.VMEM((BLOCKS, SLOTS, TOK), BF),
            pltpu.VMEM((BLOCKS, SLOTS, 128), F32),
            pltpu.VMEM((3, 4, BLOCKS * CAP, FFQ), BF),
            pltpu.SemaphoreType.DMA((3, BLOCKS)),
            pltpu.SemaphoreType.DMA((6,)),
            pltpu.SemaphoreType.DMA((3,)),
            pltpu.SemaphoreType.DMA((3,)),
        ],
        compiler_params=pltpu.CompilerParams(vmem_limit_bytes=60 << 20),
        name="experts",
    )(place, eids, tok, own[0], partner[0], own[1], partner[1], own[2], partner[2])
    return out[:12], out[12:]


def grads_kernel(*refs):
    x_ref, g_ref, dg_ref, du_ref, ha_ref = refs[:5]
    add = refs[5:-3]
    outs = refs[-3:]
    dg, du, ha = dg_ref[0], du_ref[0], ha_ref[0]
    for y in range(4):
        x = x_ref[:, y].reshape(BLOCKS * CAP, QW)
        g = g_ref[:, y].reshape(BLOCKS * CAP, QW)
        rows = pl.ds(y * QW, QW)
        where = ((0, rows), (0, rows), (0, slice(None), rows))
        parts = (dot(x, dg, 0, 0), dot(x, du, 0, 0), dot(ha, g, 0, 0))
        for n in range(3):
            part = parts[n]
            if add:
                part = part + add[n][where[n]].astype(F32)
            outs[n][where[n]] = part.astype(BF)


def run_grads(kept, first, add=()):
    x, g, dg, du, ha = kept
    rows = pl.BlockSpec((BLOCKS, 4, CAP, QW), lambda k: (0, 0, k + first, 0))
    hidden = pl.BlockSpec((1, BLOCKS * CAP, FFQ), lambda k: (k + first, 0, 0))
    shapes = [(2, 2048, FFQ), (2, 2048, FFQ), (2, FFQ, 2048)]
    grads = [pl.BlockSpec((1,) + s[1:], lambda k: (k, 0, 0)) for s in shapes]
    return pl.pallas_call(
        grads_kernel,
        grid=(2,),
        out_shape=[jax.ShapeDtypeStruct(s, BF) for s in shapes],
        in_specs=[rows, rows, hidden, hidden, hidden] + grads[: len(add)],
        out_specs=grads,
        compiler_params=pltpu.CompilerParams(vmem_limit_bytes=56 << 20),
        name="grads",
    )(x, g, dg, du, ha, *add)


def add_up(parts):
    total = parts[0].astype(F32)
    for p in parts[1:]:
        total = total + p.astype(F32)
    return total


def scatter_sum(slabs):
    orders = (("x", "z", "y"), ("z", "y", "x"), ("y", "x", "z"))
    state = [slabs[0:4], slabs[4:8], slabs[8:12]]
    for stage in range(3):
        got = []
        for n in range(3):
            axis = orders[n][stage]
            got.append([state[n][0]] + [shift(state[n][s], axis, s) for s in (1, 2, 3)])
        sums = [add_up(g) for g in got]
        if stage == 2:
            return jnp.concatenate(sums, axis=0)
        sums = [s.astype(BF) for s in sums]
        state = [[s[i] for i in range(4)] for s in sums]


def attention_backward(query, key, value, attn_grad, prefix, suffix, scale):
    block = query.shape[0]
    causal = jnp.arange(block)[:, None] >= jnp.arange(block)[None, :]
    score_grad = jnp.einsum("thj,shj->hts", attn_grad, value, precision=HIGHEST)
    score_grad = jnp.where(causal[None], score_grad, 0.0)
    score_match = jnp.einsum("thi,shi->hts", query, key, precision=HIGHEST)
    score_match = jnp.where(causal[None], score_match, 0.0)
    grad_query = jnp.einsum("hts,shi->thi", score_grad, key, precision=HIGHEST)
    grad_query = grad_query + jnp.einsum("thj,hij->thi", attn_grad, prefix, precision=HIGHEST)
    grad_key = jnp.einsum("hts,thi->shi", score_grad, query, precision=HIGHEST)
    grad_key = grad_key + jnp.einsum("shj,hij->shi", value, suffix, precision=HIGHEST)
    grad_value = jnp.einsum("hts,thj->shj", score_match, attn_grad, precision=HIGHEST)
    grad_value = grad_value + jnp.einsum("shi,hij->shj", key, suffix, precision=HIGHEST)
    return grad_query * scale, grad_key * scale, grad_value * scale


def pack_tokens(hidden_in, out_grad, expert_ids, route_weights):
    high = lax.reduce_precision(route_weights, 8, 7)
    low = route_weights - high
    rows = jnp.concatenate(
        [expert_ids.T.astype(BF), high.T.astype(BF), low.T.astype(BF), jnp.zeros((8, TOK), BF)],
        axis=0,
    )
    info = jnp.concatenate([rows[0:16], rows[16:32], jnp.zeros((INFO, 256), BF)], axis=1)
    return jnp.concatenate([hidden_in, out_grad.astype(BF), info], axis=0)


def per_device(
    hidden_in,
    out_grad,
    expert_ids,
    route_weights,
    w_gate,
    w_up,
    w_down,
    query_in,
    key_in,
    value_in,
    state_before,
    grad_after,
):
    tokens = query_in.shape[0]
    heads = query_in.shape[1] // HD
    split = (tokens, heads, HD)
    query, key, value = (a.reshape(split) for a in (query_in, key_in, value_in))
    px, pz, pc, py = (lax.axis_index(a) for a in ("x", "z", "c", "y"))
    own = (w_gate, w_up, w_down)
    partner = tuple(swap(w) for w in own)
    packed = pack_tokens(hidden_in, out_grad, expert_ids, route_weights)
    tok = lax.all_gather(packed, PLANE)
    place = jnp.stack([px, pz, py, pc]).astype(jnp.int32)
    first = 4 * (px * 4 + pz)
    eids = jnp.stack(
        [first + 2 * pc, first + 2 * pc + 1, first + 2 - 2 * pc, first + 3 - 2 * pc]
    ).astype(jnp.int32)
    slabs, kept = run_experts(place, eids, tok, own, partner)
    others = run_grads(kept, 2)
    moe_grad = scatter_sum(slabs)
    grads = run_grads(kept, 0, tuple(swap(g) for g in others))

    kv_local = jnp.einsum("shi,shj->hij", key, value, precision=HIGHEST)
    prefix = entering(kv_local, False) + state_before
    attn_grad = (out_grad + moe_grad).reshape(split)
    qd_local = jnp.einsum("thi,thj->hij", query, attn_grad, precision=HIGHEST)
    suffix = entering(qd_local, True) + grad_after
    scale = (HD * tokens * lax.axis_size(SEQ)) ** (-0.5)
    outs = attention_backward(query, key, value, attn_grad, prefix, suffix, scale)
    return tuple(grads) + tuple(o.reshape(tokens, -1) for o in outs)


def solution(mesh):
    torus = Mesh(mesh.devices.reshape(4, 4, 2, 4), ("x", "z", "c", "y"))
    wide = P(SEQ, "y")
    return jax.shard_map(
        per_device,
        mesh=torus,
        in_specs=(
            wide,
            wide,
            P(SEQ, None),
            P(SEQ, None),
            P(SEQ, None, "y"),
            P(SEQ, None, "y"),
            P(SEQ, "y", None),
            wide,
            wide,
            wide,
            P("y", None, None),
            P("y", None, None),
        ),
        out_specs=(P(SEQ, None, "y"), P(SEQ, None, "y"), P(SEQ, "y", None), wide, wide, wide),
        check_vma=False,
    )
```
